128 devices in a mesh: blk: 4 (over z), own: 32 (over y, x, core).
Axes of the slice: x: 4, y: 4, z: 4, core: 2. Of those that a mesh axis runs over, the one named last changes fastest.
Arguments:
- blocks: bfloat16 [512, 128, 16384], P(('blk', 'own')), may hold values from -6 to 6
- user_block: int32 [512], P(('blk', 'own')), may hold values from 0 to 63, as said below
- item_block: int32 [512], P(('blk', 'own')), may hold values from 0 to 15, as said below
- word_block: int32 [512], P(('blk', 'own')), may hold values from 0 to 31, as said below
- item_factor: bfloat16 [2048, 256], P('blk')
- word_factor: bfloat16 [4096, 256], replicated
Outputs:
- user_factor: float32 [128, 64, 256], P('own', 'blk')
The draws below stay inside these ranges and needn't reach their ends.
Inputs may be any that keep to these rules, and one draw needn't show every extreme that they name: `user_block`: every user block appears exactly 8 times in the list. `item_block`: every item block appears in the list. `word_block`: every word block appears in the list.
All inputs are finite; a program needn't handle non-finite values.
Results may differ from the reference program's by a relative error of at most 0.0036.
Values may be sent and summed in bfloat16 or wider, within the bound.
A program may use at most 128 MiB of HBM per device.

```python
import jax
import jax.numpy as jnp
from jax import lax

BS = 128
R = 256
WORDS = 4096
NB_TOTAL = 512
UBLOCKS = 64
IBLOCKS = 16
ITEMS = 2048
WBLOCKS = 32


def spread_list(key, count, span):
    base = jnp.arange(count, dtype=jnp.int32) % span
    return jax.random.permutation(key, base).astype(jnp.int32)


def factor_rows(key, rows):
    key_z, key_row, key_common, key_mix, key_col = jax.random.split(key, 5)
    noise = jax.random.normal(key_z, (rows, R), jnp.float32)
    row_scale = jnp.exp(jax.random.uniform(key_row, (rows, 1), jnp.float32, 0.0, jnp.log(10.0)))
    common = jax.random.normal(key_common, (rows, 1), jnp.float32)
    mixing = jax.random.uniform(key_mix, (1, R), jnp.float32, 0.5, 1.0)
    col_scale = jnp.exp(jax.random.uniform(key_col, (1, R), jnp.float32, 0.0, jnp.log(3.0)))
    values = 0.03 * row_scale * col_scale * (noise + common * mixing)
    return values.astype(jnp.bfloat16)


def draw_user_block(key, part):
    return spread_list(jax.random.fold_in(key, 11), NB_TOTAL, UBLOCKS)


def draw_item_block(key, part):
    return spread_list(jax.random.fold_in(key, 12), NB_TOTAL, IBLOCKS)


def draw_word_block(key, part):
    return spread_list(jax.random.fold_in(key, 13), NB_TOTAL, WBLOCKS)


def draw_item_factor(key, part):
    return factor_rows(jax.random.fold_in(key, 21), ITEMS)


def draw_word_factor(key, part):
    return factor_rows(jax.random.fold_in(key, 22), WORDS)


def block_levels(key, extent, cuts, smallest, top_value):
    factor_of, own = 1.0, jax.random.fold_in(key, 6)
    for axis_at, shards_of in cuts:
        draws = jnp.exp(jax.random.uniform(jax.random.fold_in(own, axis_at), (shards_of,), jnp.float32, smallest / len(cuts), top_value / len(cuts)))
        factor_of = factor_of * jnp.repeat(draws, extent[axis_at] // shards_of).reshape([-1 if axis == axis_at else 1 for axis in range(len(extent))])
    return factor_of


def scatter_about(key, dims, deviation, most, pieces=(), kind=jnp.bfloat16):
    result = jax.random.normal(key, dims, jnp.float32) * deviation
    if len(pieces) > 0:
        result = block_levels(key, dims, pieces, -0.22, 0.18) * result
    return jnp.clip(result, min=-most, max=most).astype(kind)


def setup_inputs(seed: int = 0) -> dict:
    splits = jax.random.split(jax.random.key(seed), 7)
    return {
        "blocks": scatter_about(splits[0], (NB_TOTAL, BS, BS * BS), 1.0, 6.0, ((0, 128),)),
        "user_block": draw_user_block(jax.random.fold_in(splits[6], 71), 0),
        "item_block": draw_item_block(jax.random.fold_in(splits[6], 71), 0),
        "word_block": draw_word_block(jax.random.fold_in(splits[6], 71), 0),
        "item_factor": draw_item_factor(jax.random.fold_in(splits[6], 71), 0),
        "word_factor": draw_word_factor(jax.random.fold_in(splits[6], 71), 0),
    }


def block_term(item_factor, word_factor, block, item_id, word_id):
    item_rows = lax.dynamic_slice_in_dim(item_factor, (item_id * BS).astype(jnp.int32), BS, 0)
    word_rows = lax.dynamic_slice_in_dim(word_factor, (word_id * BS).astype(jnp.int32), BS, 0)
    khatri = item_rows.astype(jnp.float32)[:, None, :] * word_rows.astype(jnp.float32)[None, :, :]
    khatri = khatri.astype(jnp.bfloat16).reshape(BS * BS, R)
    return jnp.dot(block.astype(jnp.float32), khatri.astype(jnp.float32), preferred_element_type=jnp.float32)

def reference(blocks, user_block, item_block, word_block, item_factor, word_factor):

    def visit(total, packed):
        block, user_id, item_id, word_id = packed
        partial_rows = block_term(item_factor, word_factor, block, item_id, word_id)
        return (total.at[user_id].add(partial_rows), None)
    start_total = jnp.zeros((UBLOCKS, BS, R), jnp.float32)
    mttkrp, _ = lax.scan(visit, start_total, (blocks, user_block, item_block, word_block))
    gram_items = jnp.dot(item_factor.T.astype(jnp.float32), item_factor.astype(jnp.float32), preferred_element_type=jnp.float32)
    gram_words = jnp.dot(word_factor.T.astype(jnp.float32), word_factor.astype(jnp.float32), preferred_element_type=jnp.float32)
    gram = gram_items * gram_words
    lower = jnp.linalg.cholesky(gram)
    stacked = jnp.transpose(mttkrp, (1, 0, 2)).reshape(BS * UBLOCKS, R)
    first = jax.scipy.linalg.solve_triangular(lower, stacked.T, lower=True)
    second = jax.scipy.linalg.solve_triangular(lower.T, first, lower=False)
    return second.T.reshape(BS, UBLOCKS, R)
```

```python
import functools

import jax
import jax.numpy as jnp
from jax import lax
from jax.experimental import pallas as pl
from jax.experimental.pallas import tpu as pltpu
from jax.sharding import PartitionSpec as P

MESH = pl.DeviceIdType.MESH
PANEL = 32
SUB = 16
CHUNK = 64


def split3(x):
    high = x.astype(jnp.bfloat16)
    rest = x - high.astype(jnp.float32)
    mid = rest.astype(jnp.bfloat16)
    low = (rest - mid.astype(jnp.float32)).astype(jnp.bfloat16)
    return high, mid, low


def small_inverse(cols):
    size = len(cols)
    row = lax.broadcasted_iota(jnp.int32, cols[0].shape, 0)
    cols = list(cols)
    for p in range(size):
        here = row == p
        inv = 1.0 / jnp.broadcast_to(cols[p][p : p + 1], cols[p].shape)
        factor = jnp.where(here, inv, -cols[p] * inv)
        for j in range(size):
            if j == p:
                cols[j] = factor
            else:
                pivot_row = jnp.broadcast_to(cols[j][p : p + 1], cols[j].shape)
                cols[j] = jnp.where(here, 0.0, cols[j]) + factor * pivot_row
    return cols


def combine(cols, rows):
    reps = rows.shape[1] // cols[0].shape[1]
    total = None
    for j, col in enumerate(cols):
        wide = jnp.concatenate([col] * reps, axis=1) if reps > 1 else col
        term = wide * jnp.broadcast_to(rows[j : j + 1], rows.shape)
        total = term if total is None else total + term
    return total


def eliminate(a_ref, k):
    n = a_ref.shape[0]
    base = pl.multiple_of(k * PANEL, PANEL)
    rows = a_ref[pl.ds(base, PANEL), :]
    lane = lax.broadcasted_iota(jnp.int32, (PANEL, n), 1)
    sub = lax.broadcasted_iota(jnp.int32, (PANEL, n), 0)
    inside = (lane >= base) & (lane < base + PANEL)
    eye = jnp.where(lane - base == sub, 1.0, 0.0)
    turned = jnp.where(inside, -eye, jnp.where(lane < base, -rows, rows))
    high, mid, low = split3(turned)
    left = jnp.concatenate([high, high, high, mid, mid, low], axis=0)
    rolled = pltpu.roll(rows, (n - base) % n, 1)
    count = PANEL // SUB
    panel = [rows[s * SUB : (s + 1) * SUB] for s in range(count)]
    diag = [rolled[s * SUB : (s + 1) * SUB, :128] for s in range(count)]
    lane_s, sub_s = lane[:SUB], sub[:SUB]
    lane_d = lax.broadcasted_iota(jnp.int32, (SUB, 128), 1)
    sub_d = lax.broadcasted_iota(jnp.int32, (SUB, 128), 0)
    for s in range(count):
        first = s * SUB
        cols = [
            [jnp.broadcast_to(diag[t][:, first + j : first + j + 1], (SUB, 128)) for j in range(SUB)]
            for t in range(count)
        ]
        inverse = small_inverse(cols[s])
        at = lane_s - base - first
        own = (at >= 0) & (at < SUB)
        at_d = lane_d - first
        own_d = (at_d >= 0) & (at_d < SUB)
        last = s + 1 == count
        fresh = combine(inverse, jnp.where(own, jnp.where(at == sub_s, 1.0, 0.0), panel[s]))
        fresh_d = None
        if not last:
            fresh_d = combine(inverse, jnp.where(own_d, jnp.where(at_d == sub_d, 1.0, 0.0), diag[s]))
        for t in range(count):
            if t != s:
                panel[t] = jnp.where(own, 0.0, panel[t]) - combine(cols[t], fresh)
                if not last:
                    diag[t] = jnp.where(own_d, 0.0, diag[t]) - combine(cols[t], fresh_d)
        panel[s] = fresh
        if not last:
            diag[s] = fresh_d
    solved = jnp.concatenate(panel, axis=0)
    high, mid, low = split3(solved)
    right = jnp.concatenate([high, mid, low, high, mid, high], axis=0)
    update = lax.dot_general(left, right, (((0,), (0,)), ((), ())), preferred_element_type=jnp.float32)
    lane_f = lax.broadcasted_iota(jnp.int32, (n, n), 1)
    a_ref[...] = jnp.where((lane_f >= base) & (lane_f < base + PANEL), 0.0, a_ref[...]) - update
    a_ref[pl.ds(base, PANEL), :] = solved


def block_product(block, item_id, word_id, items, words, item_rows):
    side = block.shape[0]
    rank = words.shape[1]
    item_rows[...] = items[pl.ds(item_id * side, side), :].astype(jnp.float32)
    word_rows = words[pl.ds(word_id * side, side), :]

    def step(c, total):
        terms = []
        for j in range(CHUNK):
            row = jnp.broadcast_to(item_rows[pl.ds(c * CHUNK + j, 1), :], (side, rank))
            terms.append(word_rows * row.astype(jnp.bfloat16))
        khatri = jnp.concatenate(terms, axis=0)
        values = block[:, pl.ds(pl.multiple_of(c * CHUNK * side, CHUNK * side), CHUNK * side)]
        return total + jnp.dot(values, khatri, preferred_element_type=jnp.float32)

    return lax.fori_loop(0, side // CHUNK, step, jnp.zeros((side, rank), jnp.float32))


def gram_of(rows):
    return lax.dot_general(rows, rows, (((0,), (0,)), ((), ())), preferred_element_type=jnp.float32)


def kernel(
    groups, owners, local_u,
    user_ids, item_ids, word_ids, blocks_hbm, item_hbm, word_hbm, out_ref,
    blocks, items, words, item_rows, part, gram, send, recv, mine, theirs, ids_send, ids_recv, select,
    block_sem, word_sem, item_sem, gather_send, gather_recv, pass_send, pass_recv,
    ids_ssem, ids_rsem, rows_ssem, rows_rsem, z_send, z_recv,
):
    nblocks, side = blocks.shape[0], blocks.shape[1]
    rank = words.shape[1]
    share = side // owners
    message = nblocks * share
    halves = rank // 128
    held = item_hbm.shape[0]
    half = held // 2
    group = lax.axis_index("blk")
    owner = lax.axis_index("own")
    core = owner % 2
    sibling = owner + 1 - 2 * core

    word_copy = pltpu.make_async_copy(word_hbm, words, word_sem)
    word_copy.start()
    mine_at = pl.multiple_of(group * held, held)
    item_copy = pltpu.make_async_copy(item_hbm, items.at[pl.ds(mine_at, held)], item_sem)
    item_copy.start()

    barrier = pltpu.get_barrier_semaphore()
    for d in range(1, groups):
        pl.semaphore_signal(barrier, inc=1, device_id=((group + d) % groups, owner), device_id_type=MESH)

    def greet(d, carry):
        pl.semaphore_signal(barrier, inc=1, device_id=(group, (owner + d) % owners), device_id_type=MESH)
        return carry

    lax.fori_loop(1, owners, greet, 0)
    pl.semaphore_wait(barrier, groups - 1 + owners - 1)

    def gather_copy(d, source_group):
        start = pl.multiple_of(source_group * held + core * half, half)
        return pltpu.make_async_remote_copy(
            src_ref=item_hbm.at[pl.ds(pl.multiple_of(core * half, half), half)],
            dst_ref=items.at[pl.ds(start, half)],
            send_sem=gather_send.at[d - 1],
            recv_sem=gather_recv.at[d - 1],
            device_id=((group + d) % groups, owner),
            device_id_type=MESH,
        )

    gathers = {d: gather_copy(d, group) for d in range(1, groups)}
    for d in (2, 1, 3):
        gathers[d].start()
    for n in range(nblocks):
        pltpu.make_async_copy(blocks_hbm.at[n], blocks.at[n], block_sem.at[n]).start()

    for n in range(nblocks):
        ids_send[n * share : (n + 1) * share, :] = jnp.full((share, ids_send.shape[1]), user_ids[n], jnp.int32)
    own_ids = pltpu.make_async_copy(ids_send, ids_recv.at[owner], ids_rsem)
    own_ids.start()

    def send_ids(d, carry):
        pltpu.make_async_remote_copy(
            src_ref=ids_send, dst_ref=ids_recv.at[owner], send_sem=ids_ssem, recv_sem=ids_rsem,
            device_id=(group, (owner + d) % owners), device_id_type=MESH,
        ).start()
        return carry

    lax.fori_loop(1, owners, send_ids, 0)

    word_copy.wait()
    gram_words = gram_of(words[...])

    def pass_copy(d):
        start = pl.multiple_of((group + groups - d) % groups * held + core * half, half)
        return pltpu.make_async_remote_copy(
            src_ref=items.at[pl.ds(start, half)],
            dst_ref=items.at[pl.ds(start, half)],
            send_sem=pass_send.at[d - 1],
            recv_sem=pass_recv.at[d - 1],
            device_id=(group, sibling),
            device_id_type=MESH,
        )

    passes = {}
    for d in (1, 3, 2):
        gathers[d].wait_recv()
        passes[d] = pass_copy(d)
        passes[d].start()

    pltpu.make_async_copy(ids_recv, ids_recv, ids_rsem).wait()
    rows_in = owners * message
    rows_out = groups * share * local_u
    ids = ids_recv[...].reshape(rows_in, ids_recv.shape[2])
    parts = []
    for h in range(rows_out // 128):
        to = lax.broadcasted_iota(jnp.int32, (rows_in, 128), 1) + h * 128
        source = lax.broadcasted_iota(jnp.int32, (rows_in, 128), 0)
        to_user = to // (share * local_u) * local_u + to % local_u
        hit = (ids == to_user) & (source % share == to // local_u % share)
        parts.append(jnp.where(hit, 1.0, 0.0).astype(jnp.bfloat16))
    select[...] = jnp.concatenate(parts, axis=1).T

    item_copy.wait()
    for d in (1, 3, 2):
        passes[d].wait_recv()

    pair = 2 * share

    def row_copy(t, to):
        return pltpu.make_async_remote_copy(
            src_ref=send.at[:, pl.ds(pl.multiple_of(to * message + t * pair, pair), pair)],
            dst_ref=recv.at[:, pl.ds(pl.multiple_of(owner * message + t * pair, pair), pair)],
            send_sem=rows_ssem, recv_sem=rows_rsem,
            device_id=(group, to), device_id_type=MESH,
        )

    def product_step(n, carry):
        pltpu.make_async_copy(blocks_hbm.at[n], blocks.at[n], block_sem.at[n]).wait()
        product = block_product(blocks.at[n], item_ids[n], word_ids[n], items, words, item_rows)
        for h in range(halves):
            part[h] = product[:, h * 128 : (h + 1) * 128]
            for row in range(share):
                to_rows = pl.ds(n * share + row, owners, stride=message)
                send[h, to_rows, :] = part[h, pl.ds(row, owners, stride=share), :]

        @pl.when(n % 2 == 1)
        def _():
            def send_rows(d, inner):
                row_copy(n // 2, (owner + d) % owners).start()
                return inner

            lax.fori_loop(1, owners, send_rows, 0)

        return carry

    lax.fori_loop(0, nblocks, product_step, 0)
    mine_rows = pl.ds(pl.multiple_of(owner * message, message), message)
    pltpu.make_async_copy(send.at[:, mine_rows], recv.at[:, mine_rows], rows_rsem).start()

    gram[...] = gram_of(items[...]) * gram_words
    steps = rank // PANEL

    def eliminate_step(k, carry):
        eliminate(gram, k)
        return carry

    lax.fori_loop(0, steps // 2, eliminate_step, 0)

    pltpu.make_async_copy(recv, recv, rows_rsem).wait()
    high, mid, low = split3(jnp.concatenate([recv[h] for h in range(halves)], axis=1))
    chosen = select[...]
    total = jnp.dot(chosen, high, preferred_element_type=jnp.float32)
    total += jnp.dot(chosen, mid, preferred_element_type=jnp.float32)
    total += jnp.dot(chosen, low, preferred_element_type=jnp.float32)
    mine[...] = total
    count = share * local_u

    def z_copy(d):
        to = (group + d) % groups
        return pltpu.make_async_remote_copy(
            src_ref=mine.at[pl.ds(pl.multiple_of(to * count, count), count)],
            dst_ref=theirs.at[d - 1],
            send_sem=z_send.at[d - 1], recv_sem=z_recv.at[d - 1],
            device_id=(to, owner), device_id_type=MESH,
        )

    zs = [z_copy(d) for d in range(1, groups)]
    for z in zs:
        z.start()

    lax.fori_loop(steps // 2, steps, eliminate_step, 0)

    rows = mine[pl.ds(pl.multiple_of(group * count, count), count), :]
    for d in range(1, groups):
        zs[d - 1].wait_recv()
        rows = rows + theirs[d - 1]
    solved = jnp.dot(rows, gram[...], preferred_element_type=jnp.float32, precision=lax.Precision.HIGHEST)
    out_ref[...] = solved.reshape(out_ref.shape)

    for d in range(1, groups):
        gathers[d].wait_send()
        passes[d].wait_send()
        zs[d - 1].wait_send()
    other_ids = ids_recv.at[pl.ds(0, owners - 1)]
    pltpu.make_async_copy(other_ids, other_ids, ids_ssem).wait()
    other_rows = send.at[:, pl.ds(0, (owners - 1) * message)]
    pltpu.make_async_copy(other_rows, other_rows, rows_ssem).wait()


def solution(mesh):
    groups, owners = mesh.shape["blk"], mesh.shape["own"]

    def on_device(blocks, user_block, item_block, word_block, item_factor, word_factor):
        nblocks, side, _ = blocks.shape
        rank = item_factor.shape[1]
        share = side // owners
        message = nblocks * share
        local_u = nblocks * owners // 8
        count = share * local_u
        dma = pltpu.SemaphoreType.DMA
        smem = pl.BlockSpec(memory_space=pltpu.SMEM)
        hbm = pl.BlockSpec(memory_space=pl.ANY)
        return pl.pallas_call(
            functools.partial(kernel, groups, owners, local_u),
            out_shape=jax.ShapeDtypeStruct((share, local_u, rank), jnp.float32),
            in_specs=[smem, smem, smem, hbm, hbm, hbm],
            out_specs=pl.BlockSpec(memory_space=pltpu.VMEM),
            scratch_shapes=[
                pltpu.VMEM(blocks.shape, jnp.bfloat16),
                pltpu.VMEM((groups * item_factor.shape[0], rank), jnp.bfloat16),
                pltpu.VMEM(word_factor.shape, jnp.bfloat16),
                pltpu.VMEM((side, rank), jnp.float32),
                pltpu.VMEM((rank // 128, side, 128), jnp.float32),
                pltpu.VMEM((rank, rank), jnp.float32),
                pltpu.VMEM((rank // 128, owners * message, 128), jnp.float32),
                pltpu.VMEM((rank // 128, owners * message, 128), jnp.float32),
                pltpu.VMEM((groups * count, rank), jnp.float32),
                pltpu.VMEM((groups - 1, count, rank), jnp.float32),
                pltpu.VMEM((message, 128), jnp.int32),
                pltpu.VMEM((owners, message, 128), jnp.int32),
                pltpu.VMEM((groups * count, owners * message), jnp.bfloat16),
                dma((nblocks,)), dma, dma,
                dma((groups - 1,)), dma((groups - 1,)), dma((groups - 1,)), dma((groups - 1,)),
                dma, dma, dma, dma,
                dma((groups - 1,)), dma((groups - 1,)),
            ],
            compiler_params=pltpu.CompilerParams(
                collective_id=0, has_side_effects=True, vmem_limit_bytes=56 * 2**20
            ),
            name="als_user_update",
        )(user_block, item_block, word_block, blocks, item_factor, word_factor)

    return jax.shard_map(
        on_device,
        mesh=mesh,
        in_specs=(
            P(("blk", "own"), None, None),
            P(("blk", "own")),
            P(("blk", "own")),
            P(("blk", "own")),
            P("blk", None),
            P(),
        ),
        out_specs=P("own", "blk", None),
        check_vma=False,
    )
```

```python
import functools

import jax
import jax.numpy as jnp
from jax import lax
from jax.experimental import pallas as pl
from jax.experimental.pallas import tpu as pltpu
from jax.sharding import PartitionSpec as P

MESH = pl.DeviceIdType.MESH
PANEL = 32
SUB = 16
CHUNK = 128


def split3(x):
    high = x.astype(jnp.bfloat16)
    rest = x - high.astype(jnp.float32)
    mid = rest.astype(jnp.bfloat16)
    low = (rest - mid.astype(jnp.float32)).astype(jnp.bfloat16)
    return high, mid, low


def small_inverse(cols):
    size = len(cols)
    row = lax.broadcasted_iota(jnp.int32, cols[0].shape, 0)
    cols = list(cols)
    for p in range(size):
        here = row == p
        inv = 1.0 / jnp.broadcast_to(cols[p][p : p + 1], cols[p].shape)
        factor = jnp.where(here, inv, -cols[p] * inv)
        for j in range(size):
            if j == p:
                cols[j] = factor
            else:
                pivot_row = jnp.broadcast_to(cols[j][p : p + 1], cols[j].shape)
                cols[j] = jnp.where(here, 0.0, cols[j]) + factor * pivot_row
    return cols


def combine(cols, rows):
    reps = rows.shape[1] // cols[0].shape[1]
    total = None
    for j, col in enumerate(cols):
        wide = jnp.concatenate([col] * reps, axis=1) if reps > 1 else col
        term = wide * jnp.broadcast_to(rows[j : j + 1], rows.shape)
        total = term if total is None else total + term
    return total


def eliminate(a_ref, k):
    n = a_ref.shape[0]
    base = pl.multiple_of(k * PANEL, PANEL)
    rows = a_ref[pl.ds(base, PANEL), :]
    lane = lax.broadcasted_iota(jnp.int32, (PANEL, n), 1)
    sub = lax.broadcasted_iota(jnp.int32, (PANEL, n), 0)
    inside = (lane >= base) & (lane < base + PANEL)
    eye = jnp.where(lane - base == sub, 1.0, 0.0)
    turned = jnp.where(inside, -eye, jnp.where(lane < base, -rows, rows))
    high, mid, low = split3(turned)
    left = jnp.concatenate([high, high, high, mid, mid, low], axis=0)
    rolled = pltpu.roll(rows, (n - base) % n, 1)
    count = PANEL // SUB
    panel = [rows[s * SUB : (s + 1) * SUB] for s in range(count)]
    diag = [rolled[s * SUB : (s + 1) * SUB, :128] for s in range(count)]
    lane_s, sub_s = lane[:SUB], sub[:SUB]
    lane_d = lax.broadcasted_iota(jnp.int32, (SUB, 128), 1)
    sub_d = lax.broadcasted_iota(jnp.int32, (SUB, 128), 0)
    for s in range(count):
        first = s * SUB
        cols = [
            [jnp.broadcast_to(diag[t][:, first + j : first + j + 1], (SUB, 128)) for j in range(SUB)]
            for t in range(count)
        ]
        inverse = small_inverse(cols[s])
        at = lane_s - base - first
        own = (at >= 0) & (at < SUB)
        at_d = lane_d - first
        own_d = (at_d >= 0) & (at_d < SUB)
        last = s + 1 == count
        fresh = combine(inverse, jnp.where(own, jnp.where(at == sub_s, 1.0, 0.0), panel[s]))
        fresh_d = None
        if not last:
            fresh_d = combine(inverse, jnp.where(own_d, jnp.where(at_d == sub_d, 1.0, 0.0), diag[s]))
        for t in range(count):
            if t != s:
                panel[t] = jnp.where(own, 0.0, panel[t]) - combine(cols[t], fresh)
                if not last:
                    diag[t] = jnp.where(own_d, 0.0, diag[t]) - combine(cols[t], fresh_d)
        panel[s] = fresh
        if not last:
            diag[s] = fresh_d
    solved = jnp.concatenate(panel, axis=0)
    high, mid, low = split3(solved)
    right = jnp.concatenate([high, mid, low, high, mid, high], axis=0)
    update = lax.dot_general(left, right, (((0,), (0,)), ((), ())), preferred_element_type=jnp.float32)
    lane_f = lax.broadcasted_iota(jnp.int32, (n, n), 1)
    a_ref[...] = jnp.where((lane_f >= base) & (lane_f < base + PANEL), 0.0, a_ref[...]) - update
    a_ref[pl.ds(base, PANEL), :] = solved


def block_product(block, item_id, word_id, items, words, item_rows):
    side = block.shape[0]
    rank = words.shape[1]
    item_rows[...] = items[pl.ds(item_id * side, side), :].astype(jnp.float32)
    word_rows = words[pl.ds(word_id * side, side), :]

    def step(c, total):
        terms = []
        for j in range(CHUNK):
            row = jnp.broadcast_to(item_rows[pl.ds(c * CHUNK + j, 1), :], (side, rank))
            terms.append(word_rows * row.astype(jnp.bfloat16))
        khatri = jnp.concatenate(terms, axis=0)
        values = block[:, pl.ds(pl.multiple_of(c * CHUNK * side, CHUNK * side), CHUNK * side)]
        return total + jnp.dot(values, khatri, preferred_element_type=jnp.float32)

    return lax.fori_loop(0, side // CHUNK, step, jnp.zeros((side, rank), jnp.float32))


def gram_of(rows):
    return lax.dot_general(rows, rows, (((0,), (0,)), ((), ())), preferred_element_type=jnp.float32)


def kernel(
    groups, owners, local_u,
    user_ids, item_ids, word_ids, blocks_hbm, item_hbm, word_hbm, out_ref,
    blocks, items, words, item_rows, part, gram, send, recv, mine, theirs, ids_send, ids_recv, select,
    block_sem, word_sem, item_sem, gather_send, gather_recv, pass_send, pass_recv,
    ids_ssem, ids_rsem, rows_ssem, rows_rsem, z_send, z_recv,
):
    nblocks, side = blocks.shape[0], blocks.shape[1]
    rank = words.shape[1]
    share = side // owners
    message = nblocks * share
    halves = rank // 128
    held = item_hbm.shape[0]
    half = held // 2
    group = lax.axis_index("blk")
    owner = lax.axis_index("own")
    core = owner % 2
    sibling = owner + 1 - 2 * core

    word_copy = pltpu.make_async_copy(word_hbm, words, word_sem)
    word_copy.start()
    mine_at = pl.multiple_of(group * held, held)
    item_copy = pltpu.make_async_copy(item_hbm, items.at[pl.ds(mine_at, held)], item_sem)
    item_copy.start()

    barrier = pltpu.get_barrier_semaphore()
    for d in range(1, groups):
        pl.semaphore_signal(barrier, inc=1, device_id=((group + d) % groups, owner), device_id_type=MESH)

    def greet(d, carry):
        pl.semaphore_signal(barrier, inc=1, device_id=(group, (owner + d) % owners), device_id_type=MESH)
        return carry

    lax.fori_loop(1, owners, greet, 0)
    for n in range(nblocks):
        pltpu.make_async_copy(blocks_hbm.at[n], blocks.at[n], block_sem.at[n]).start()
    pl.semaphore_wait(barrier, groups - 1 + owners - 1)

    def gather_copy(d, source_group):
        start = pl.multiple_of(source_group * held + core * half, half)
        return pltpu.make_async_remote_copy(
            src_ref=item_hbm.at[pl.ds(pl.multiple_of(core * half, half), half)],
            dst_ref=items.at[pl.ds(start, half)],
            send_sem=gather_send.at[d - 1],
            recv_sem=gather_recv.at[d - 1],
            device_id=((group + d) % groups, owner),
            device_id_type=MESH,
        )

    gathers = {d: gather_copy(d, group) for d in range(1, groups)}
    for d in (2, 1, 3):
        gathers[d].start()

    for n in range(nblocks):
        ids_send[n * share : (n + 1) * share, :] = jnp.full((share, ids_send.shape[1]), user_ids[n], jnp.int32)
    own_ids = pltpu.make_async_copy(ids_send, ids_recv.at[owner], ids_rsem)
    own_ids.start()

    def send_ids(d, carry):
        pltpu.make_async_remote_copy(
            src_ref=ids_send, dst_ref=ids_recv.at[owner], send_sem=ids_ssem, recv_sem=ids_rsem,
            device_id=(group, (owner + d) % owners), device_id_type=MESH,
        ).start()
        return carry

    lax.fori_loop(1, owners, send_ids, 0)

    word_copy.wait()
    gram_words = gram_of(words[...])

    def pass_copy(d):
        start = pl.multiple_of((group + groups - d) % groups * held + core * half, half)
        return pltpu.make_async_remote_copy(
            src_ref=items.at[pl.ds(start, half)],
            dst_ref=items.at[pl.ds(start, half)],
            send_sem=pass_send.at[d - 1],
            recv_sem=pass_recv.at[d - 1],
            device_id=(group, sibling),
            device_id_type=MESH,
        )

    passes = {}
    for d in (1, 3, 2):
        gathers[d].wait_recv()
        passes[d] = pass_copy(d)
        passes[d].start()

    item_copy.wait()
    for d in (1, 3, 2):
        passes[d].wait_recv()

    pair = 2 * share

    def row_copy(t, to):
        return pltpu.make_async_remote_copy(
            src_ref=send.at[:, pl.ds(pl.multiple_of(to * message + t * pair, pair), pair)],
            dst_ref=recv.at[:, pl.ds(pl.multiple_of(owner * message + t * pair, pair), pair)],
            send_sem=rows_ssem, recv_sem=rows_rsem,
            device_id=(group, to), device_id_type=MESH,
        )

    def product_step(n, carry):
        pltpu.make_async_copy(blocks_hbm.at[n], blocks.at[n], block_sem.at[n]).wait()
        product = block_product(blocks.at[n], item_ids[n], word_ids[n], items, words, item_rows)
        for h in range(halves):
            part[h] = product[:, h * 128 : (h + 1) * 128]
            for row in range(share):
                to_rows = pl.ds(n * share + row, owners, stride=message)
                send[h, to_rows, :] = part[h, pl.ds(row, owners, stride=share), :]

        @pl.when(n % 2 == 1)
        def _():
            def send_rows(d, inner):
                row_copy(n // 2, (owner + d) % owners).start()
                return inner

            lax.fori_loop(1, owners, send_rows, 0)

        return carry

    lax.fori_loop(0, nblocks, product_step, 0)
    mine_rows = pl.ds(pl.multiple_of(owner * message, message), message)
    pltpu.make_async_copy(send.at[:, mine_rows], recv.at[:, mine_rows], rows_rsem).start()

    pltpu.make_async_copy(ids_recv, ids_recv, ids_rsem).wait()
    rows_in = owners * message
    rows_out = groups * share * local_u
    ids = ids_recv[...].reshape(rows_in, ids_recv.shape[2])
    parts = []
    for h in range(rows_out // 128):
        to = lax.broadcasted_iota(jnp.int32, (rows_in, 128), 1) + h * 128
        source = lax.broadcasted_iota(jnp.int32, (rows_in, 128), 0)
        to_user = to // (share * local_u) * local_u + to % local_u
        hit = (ids == to_user) & (source % share == to // local_u % share)
        parts.append(jnp.where(hit, 1.0, 0.0).astype(jnp.bfloat16))
    select[...] = jnp.concatenate(parts, axis=1).T

    gram[...] = gram_of(items[...]) * gram_words
    steps = rank // PANEL

    def eliminate_step(k, carry):
        eliminate(gram, k)
        return carry

    lax.fori_loop(0, steps // 2, eliminate_step, 0)

    pltpu.make_async_copy(recv, recv, rows_rsem).wait()
    high, mid, low = split3(jnp.concatenate([recv[h] for h in range(halves)], axis=1))
    chosen = select[...]
    total = jnp.dot(chosen, high, preferred_element_type=jnp.float32)
    total += jnp.dot(chosen, mid, preferred_element_type=jnp.float32)
    total += jnp.dot(chosen, low, preferred_element_type=jnp.float32)
    mine[...] = total
    count = share * local_u

    def z_copy(d):
        to = (group + d) % groups
        return pltpu.make_async_remote_copy(
            src_ref=mine.at[pl.ds(pl.multiple_of(to * count, count), count)],
            dst_ref=theirs.at[d - 1],
            send_sem=z_send.at[d - 1], recv_sem=z_recv.at[d - 1],
            device_id=(to, owner), device_id_type=MESH,
        )

    zs = [z_copy(d) for d in range(1, groups)]
    for z in zs:
        z.start()

    lax.fori_loop(steps // 2, steps, eliminate_step, 0)

    rows = mine[pl.ds(pl.multiple_of(group * count, count), count), :]
    for d in range(1, groups):
        zs[d - 1].wait_recv()
        rows = rows + theirs[d - 1]
    solved = jnp.dot(rows, gram[...], preferred_element_type=jnp.float32, precision=lax.Precision.HIGHEST)
    out_ref[...] = solved.reshape(out_ref.shape)

    for d in range(1, groups):
        gathers[d].wait_send()
        passes[d].wait_send()
        zs[d - 1].wait_send()
    other_ids = ids_recv.at[pl.ds(0, owners - 1)]
    pltpu.make_async_copy(other_ids, other_ids, ids_ssem).wait()
    other_rows = send.at[:, pl.ds(0, (owners - 1) * message)]
    pltpu.make_async_copy(other_rows, other_rows, rows_ssem).wait()


def solution(mesh):
    groups, owners = mesh.shape["blk"], mesh.shape["own"]

    def on_device(blocks, user_block, item_block, word_block, item_factor, word_factor):
        nblocks, side, _ = blocks.shape
        rank = item_factor.shape[1]
        share = side // owners
        message = nblocks * share
        local_u = nblocks * owners // 8
        count = share * local_u
        dma = pltpu.SemaphoreType.DMA
        smem = pl.BlockSpec(memory_space=pltpu.SMEM)
        hbm = pl.BlockSpec(memory_space=pl.ANY)
        return pl.pallas_call(
            functools.partial(kernel, groups, owners, local_u),
            out_shape=jax.ShapeDtypeStruct((share, local_u, rank), jnp.float32),
            in_specs=[smem, smem, smem, hbm, hbm, hbm],
            out_specs=pl.BlockSpec(memory_space=pltpu.VMEM),
            scratch_shapes=[
                pltpu.VMEM(blocks.shape, jnp.bfloat16),
                pltpu.VMEM((groups * item_factor.shape[0], rank), jnp.bfloat16),
                pltpu.VMEM(word_factor.shape, jnp.bfloat16),
                pltpu.VMEM((side, rank), jnp.float32),
                pltpu.VMEM((rank // 128, side, 128), jnp.float32),
                pltpu.VMEM((rank, rank), jnp.float32),
                pltpu.VMEM((rank // 128, owners * message, 128), jnp.float32),
                pltpu.VMEM((rank // 128, owners * message, 128), jnp.float32),
                pltpu.VMEM((groups * count, rank), jnp.float32),
                pltpu.VMEM((groups - 1, count, rank), jnp.float32),
                pltpu.VMEM((message, 128), jnp.int32),
                pltpu.VMEM((owners, message, 128), jnp.int32),
                pltpu.VMEM((groups * count, owners * message), jnp.bfloat16),
                dma((nblocks,)), dma, dma,
                dma((groups - 1,)), dma((groups - 1,)), dma((groups - 1,)), dma((groups - 1,)),
                dma, dma, dma, dma,
                dma((groups - 1,)), dma((groups - 1,)),
            ],
            compiler_params=pltpu.CompilerParams(
                collective_id=0, has_side_effects=True, vmem_limit_bytes=56 * 2**20
            ),
            name="als_user_update",
        )(user_block, item_block, word_block, blocks, item_factor, word_factor)

    return jax.shard_map(
        on_device,
        mesh=mesh,
        in_specs=(
            P(("blk", "own"), None, None),
            P(("blk", "own")),
            P(("blk", "own")),
            P(("blk", "own")),
            P("blk", None),
            P(),
        ),
        out_specs=P("own", "blk", None),
        check_vma=False,
    )
```

```python
import functools

import jax
import jax.numpy as jnp
from jax import lax
from jax.experimental import pallas as pl
from jax.experimental.pallas import tpu as pltpu
from jax.sharding import PartitionSpec as P

MESH = pl.DeviceIdType.MESH
PANEL = 32
SUB = 16
CHUNK = 128


def split3(x):
    high = x.astype(jnp.bfloat16)
    rest = x - high.astype(jnp.float32)
    mid = rest.astype(jnp.bfloat16)
    low = (rest - mid.astype(jnp.float32)).astype(jnp.bfloat16)
    return high, mid, low


def small_inverse(cols):
    size = len(cols)
    row = lax.broadcasted_iota(jnp.int32, cols[0].shape, 0)
    cols = list(cols)
    for p in range(size):
        here = row == p
        inv = 1.0 / jnp.broadcast_to(cols[p][p : p + 1], cols[p].shape)
        factor = jnp.where(here, inv, -cols[p] * inv)
        for j in range(size):
            if j == p:
                cols[j] = factor
            else:
                pivot_row = jnp.broadcast_to(cols[j][p : p + 1], cols[j].shape)
                cols[j] = jnp.where(here, 0.0, cols[j]) + factor * pivot_row
    return cols


def combine(cols, rows):
    reps = rows.shape[1] // cols[0].shape[1]
    total = None
    for j, col in enumerate(cols):
        wide = jnp.concatenate([col] * reps, axis=1) if reps > 1 else col
        term = wide * jnp.broadcast_to(rows[j : j + 1], rows.shape)
        total = term if total is None else total + term
    return total


def eliminate(a_ref, k):
    n = a_ref.shape[0]
    base = pl.multiple_of(k * PANEL, PANEL)
    rows = a_ref[pl.ds(base, PANEL), :]
    lane = lax.broadcasted_iota(jnp.int32, (PANEL, n), 1)
    sub = lax.broadcasted_iota(jnp.int32, (PANEL, n), 0)
    inside = (lane >= base) & (lane < base + PANEL)
    eye = jnp.where(lane - base == sub, 1.0, 0.0)
    turned = jnp.where(inside, -eye, jnp.where(lane < base, -rows, rows))
    high, mid, low = split3(turned)
    left = jnp.concatenate([high, high, high, mid, mid, low], axis=0)
    rolled = pltpu.roll(rows, (n - base) % n, 1)
    count = PANEL // SUB
    panel = [rows[s * SUB : (s + 1) * SUB] for s in range(count)]
    diag = [rolled[s * SUB : (s + 1) * SUB, :128] for s in range(count)]
    lane_s, sub_s = lane[:SUB], sub[:SUB]
    lane_d = lax.broadcasted_iota(jnp.int32, (SUB, 128), 1)
    sub_d = lax.broadcasted_iota(jnp.int32, (SUB, 128), 0)
    for s in range(count):
        first = s * SUB
        cols = [
            [jnp.broadcast_to(diag[t][:, first + j : first + j + 1], (SUB, 128)) for j in range(SUB)]
            for t in range(count)
        ]
        inverse = small_inverse(cols[s])
        at = lane_s - base - first
        own = (at >= 0) & (at < SUB)
        at_d = lane_d - first
        own_d = (at_d >= 0) & (at_d < SUB)
        last = s + 1 == count
        fresh = combine(inverse, jnp.where(own, jnp.where(at == sub_s, 1.0, 0.0), panel[s]))
        fresh_d = None
        if not last:
            fresh_d = combine(inverse, jnp.where(own_d, jnp.where(at_d == sub_d, 1.0, 0.0), diag[s]))
        for t in range(count):
            if t != s:
                panel[t] = jnp.where(own, 0.0, panel[t]) - combine(cols[t], fresh)
                if not last:
                    diag[t] = jnp.where(own_d, 0.0, diag[t]) - combine(cols[t], fresh_d)
        panel[s] = fresh
        if not last:
            diag[s] = fresh_d
    solved = jnp.concatenate(panel, axis=0)
    high, mid, low = split3(solved)
    right = jnp.concatenate([high, mid, low, high, mid, high], axis=0)
    update = lax.dot_general(left, right, (((0,), (0,)), ((), ())), preferred_element_type=jnp.float32)
    lane_f = lax.broadcasted_iota(jnp.int32, (n, n), 1)
    a_ref[...] = jnp.where((lane_f >= base) & (lane_f < base + PANEL), 0.0, a_ref[...]) - update
    a_ref[pl.ds(base, PANEL), :] = solved


def block_product(block, item_id, word_id, items, words, item_rows):
    side = block.shape[0]
    rank = words.shape[1]
    item_rows[...] = items[pl.ds(item_id * side, side), :].astype(jnp.float32)
    word_rows = words[pl.ds(word_id * side, side), :]

    def step(c, total):
        terms = []
        for j in range(CHUNK):
            row = jnp.broadcast_to(item_rows[pl.ds(c * CHUNK + j, 1), :], (side, rank))
            terms.append(word_rows * row.astype(jnp.bfloat16))
        khatri = jnp.concatenate(terms, axis=0)
        values = block[:, pl.ds(pl.multiple_of(c * CHUNK * side, CHUNK * side), CHUNK * side)]
        return total + jnp.dot(values, khatri, preferred_element_type=jnp.float32)

    return lax.fori_loop(0, side // CHUNK, step, jnp.zeros((side, rank), jnp.float32))


def gram_of(rows):
    return lax.dot_general(rows, rows, (((0,), (0,)), ((), ())), preferred_element_type=jnp.float32)


def kernel(
    groups, owners, local_u,
    user_ids, item_ids, word_ids, blocks_hbm, item_hbm, word_hbm, out_ref,
    blocks, items, words, item_rows, part, gram, send, recv, mine, theirs, ids_send, ids_recv, select,
    block_sem, word_sem, item_sem, gather_send, gather_recv, pass_send, pass_recv,
    ids_ssem, ids_rsem, rows_ssem, rows_rsem, z_send, z_recv,
):
    nblocks, side = blocks.shape[0], blocks.shape[1]
    rank = words.shape[1]
    share = side // owners
    message = nblocks * share
    halves = rank // 128
    held = item_hbm.shape[0]
    half = held // 2
    group = lax.axis_index("blk")
    owner = lax.axis_index("own")
    core = owner % 2
    sibling = owner + 1 - 2 * core

    word_copy = pltpu.make_async_copy(word_hbm, words, word_sem)
    word_copy.start()
    mine_at = pl.multiple_of(group * held, held)
    item_copy = pltpu.make_async_copy(item_hbm, items.at[pl.ds(mine_at, held)], item_sem)
    item_copy.start()

    barrier = pltpu.get_barrier_semaphore()
    for d in range(1, groups):
        pl.semaphore_signal(barrier, inc=1, device_id=((group + d) % groups, owner), device_id_type=MESH)

    def greet(d, carry):
        pl.semaphore_signal(barrier, inc=1, device_id=(group, (owner + d) % owners), device_id_type=MESH)
        return carry

    lax.fori_loop(1, owners, greet, 0)
    for n in range(nblocks):
        pltpu.make_async_copy(blocks_hbm.at[n], blocks.at[n], block_sem.at[n]).start()
    pl.semaphore_wait(barrier, groups - 1 + owners - 1)

    quarter = half // 2
    pieces = ((1, 0, half), (3, 0, half), (2, 0, quarter), (2, quarter, quarter))

    def gather_copy(i):
        d, first, length = pieces[i]
        start = pl.multiple_of(group * held + core * half + first, quarter)
        return pltpu.make_async_remote_copy(
            src_ref=item_hbm.at[pl.ds(pl.multiple_of(core * half + first, quarter), length)],
            dst_ref=items.at[pl.ds(start, length)],
            send_sem=gather_send.at[i],
            recv_sem=gather_recv.at[i],
            device_id=((group + d) % groups, owner),
            device_id_type=MESH,
        )

    gathers = [gather_copy(i) for i in range(len(pieces))]
    for i in (2, 0, 1, 3):
        gathers[i].start()

    for n in range(nblocks):
        ids_send[n * share : (n + 1) * share, :] = jnp.full((share, ids_send.shape[1]), user_ids[n], jnp.int32)
    own_ids = pltpu.make_async_copy(ids_send, ids_recv.at[owner], ids_rsem)
    own_ids.start()

    def send_ids(d, carry):
        pltpu.make_async_remote_copy(
            src_ref=ids_send, dst_ref=ids_recv.at[owner], send_sem=ids_ssem, recv_sem=ids_rsem,
            device_id=(group, (owner + d) % owners), device_id_type=MESH,
        ).start()
        return carry

    lax.fori_loop(1, owners, send_ids, 0)

    word_copy.wait()
    gram_words = gram_of(words[...])

    def pass_copy(i):
        d, first, length = pieces[i]
        start = pl.multiple_of((group + groups - d) % groups * held + core * half + first, quarter)
        return pltpu.make_async_remote_copy(
            src_ref=items.at[pl.ds(start, length)],
            dst_ref=items.at[pl.ds(start, length)],
            send_sem=pass_send.at[i],
            recv_sem=pass_recv.at[i],
            device_id=(group, sibling),
            device_id_type=MESH,
        )

    passes = [pass_copy(i) for i in range(len(pieces))]
    for gather, shared in zip(gathers, passes):
        gather.wait_recv()
        shared.start()

    item_copy.wait()
    for shared in passes:
        shared.wait_recv()

    pair = 2 * share

    def row_copy(t, to):
        return pltpu.make_async_remote_copy(
            src_ref=send.at[:, pl.ds(pl.multiple_of(to * message + t * pair, pair), pair)],
            dst_ref=recv.at[:, pl.ds(pl.multiple_of(owner * message + t * pair, pair), pair)],
            send_sem=rows_ssem, recv_sem=rows_rsem,
            device_id=(group, to), device_id_type=MESH,
        )

    def product_step(n, carry):
        pltpu.make_async_copy(blocks_hbm.at[n], blocks.at[n], block_sem.at[n]).wait()
        product = block_product(blocks.at[n], item_ids[n], word_ids[n], items, words, item_rows)
        for h in range(halves):
            part[h] = product[:, h * 128 : (h + 1) * 128]
            for row in range(share):
                to_rows = pl.ds(n * share + row, owners, stride=message)
                send[h, to_rows, :] = part[h, pl.ds(row, owners, stride=share), :]

        @pl.when(n % 2 == 1)
        def _():
            def send_rows(d, inner):
                row_copy(n // 2, (owner + d) % owners).start()
                return inner

            lax.fori_loop(1, owners, send_rows, 0)

        return carry

    lax.fori_loop(0, nblocks, product_step, 0)
    mine_rows = pl.ds(pl.multiple_of(owner * message, message), message)
    pltpu.make_async_copy(send.at[:, mine_rows], recv.at[:, mine_rows], rows_rsem).start()

    pltpu.make_async_copy(ids_recv, ids_recv, ids_rsem).wait()
    rows_in = owners * message
    rows_out = groups * share * local_u
    ids = ids_recv[...].reshape(rows_in, ids_recv.shape[2])
    parts = []
    for h in range(rows_out // 128):
        to = lax.broadcasted_iota(jnp.int32, (rows_in, 128), 1) + h * 128
        source = lax.broadcasted_iota(jnp.int32, (rows_in, 128), 0)
        to_user = to // (share * local_u) * local_u + to % local_u
        hit = (ids == to_user) & (source % share == to // local_u % share)
        parts.append(jnp.where(hit, 1.0, 0.0).astype(jnp.bfloat16))
    select[...] = jnp.concatenate(parts, axis=1).T

    gram[...] = gram_of(items[...]) * gram_words
    steps = rank // PANEL

    def eliminate_step(k, carry):
        eliminate(gram, k)
        return carry

    lax.fori_loop(0, steps // 2, eliminate_step, 0)

    pltpu.make_async_copy(recv, recv, rows_rsem).wait()
    high, mid, low = split3(jnp.concatenate([recv[h] for h in range(halves)], axis=1))
    chosen = select[...]
    total = jnp.dot(chosen, high, preferred_element_type=jnp.float32)
    total += jnp.dot(chosen, mid, preferred_element_type=jnp.float32)
    total += jnp.dot(chosen, low, preferred_element_type=jnp.float32)
    mine[...] = total
    count = share * local_u

    def z_copy(d):
        to = (group + d) % groups
        return pltpu.make_async_remote_copy(
            src_ref=mine.at[pl.ds(pl.multiple_of(to * count, count), count)],
            dst_ref=theirs.at[d - 1],
            send_sem=z_send.at[d - 1], recv_sem=z_recv.at[d - 1],
            device_id=(to, owner), device_id_type=MESH,
        )

    zs = [z_copy(d) for d in range(1, groups)]
    for z in zs:
        z.start()

    lax.fori_loop(steps // 2, steps, eliminate_step, 0)

    rows = mine[pl.ds(pl.multiple_of(group * count, count), count), :]
    for d in range(1, groups):
        zs[d - 1].wait_recv()
        rows = rows + theirs[d - 1]
    solved = jnp.dot(rows, gram[...], preferred_element_type=jnp.float32, precision=lax.Precision.HIGHEST)
    out_ref[...] = solved.reshape(out_ref.shape)

    for sent in gathers + passes + zs:
        sent.wait_send()
    other_ids = ids_recv.at[pl.ds(0, owners - 1)]
    pltpu.make_async_copy(other_ids, other_ids, ids_ssem).wait()
    other_rows = send.at[:, pl.ds(0, (owners - 1) * message)]
    pltpu.make_async_copy(other_rows, other_rows, rows_ssem).wait()


def solution(mesh):
    groups, owners = mesh.shape["blk"], mesh.shape["own"]

    def on_device(blocks, user_block, item_block, word_block, item_factor, word_factor):
        nblocks, side, _ = blocks.shape
        rank = item_factor.shape[1]
        share = side // owners
        message = nblocks * share
        local_u = nblocks * owners // 8
        count = share * local_u
        dma = pltpu.SemaphoreType.DMA
        smem = pl.BlockSpec(memory_space=pltpu.SMEM)
        hbm = pl.BlockSpec(memory_space=pl.ANY)
        return pl.pallas_call(
            functools.partial(kernel, groups, owners, local_u),
            out_shape=jax.ShapeDtypeStruct((share, local_u, rank), jnp.float32),
            in_specs=[smem, smem, smem, hbm, hbm, hbm],
            out_specs=pl.BlockSpec(memory_space=pltpu.VMEM),
            scratch_shapes=[
                pltpu.VMEM(blocks.shape, jnp.bfloat16),
                pltpu.VMEM((groups * item_factor.shape[0], rank), jnp.bfloat16),
                pltpu.VMEM(word_factor.shape, jnp.bfloat16),
                pltpu.VMEM((side, rank), jnp.float32),
                pltpu.VMEM((rank // 128, side, 128), jnp.float32),
                pltpu.VMEM((rank, rank), jnp.float32),
                pltpu.VMEM((rank // 128, owners * message, 128), jnp.float32),
                pltpu.VMEM((rank // 128, owners * message, 128), jnp.float32),
                pltpu.VMEM((groups * count, rank), jnp.float32),
                pltpu.VMEM((groups - 1, count, rank), jnp.float32),
                pltpu.VMEM((message, 128), jnp.int32),
                pltpu.VMEM((owners, message, 128), jnp.int32),
                pltpu.VMEM((groups * count, owners * message), jnp.bfloat16),
                dma((nblocks,)), dma, dma,
                dma((4,)), dma((4,)), dma((4,)), dma((4,)),
                dma, dma, dma, dma,
                dma((groups - 1,)), dma((groups - 1,)),
            ],
            compiler_params=pltpu.CompilerParams(
                collective_id=0, has_side_effects=True, vmem_limit_bytes=56 * 2**20
            ),
            name="als_user_update",
        )(user_block, item_block, word_block, blocks, item_factor, word_factor)

    return jax.shard_map(
        on_device,
        mesh=mesh,
        in_specs=(
            P(("blk", "own"), None, None),
            P(("blk", "own")),
            P(("blk", "own")),
            P(("blk", "own")),
            P("blk", None),
            P(),
        ),
        out_specs=P("own", "blk", None),
        check_vma=False,
    )
```

```python
import functools

import jax
import jax.numpy as jnp
from jax import lax
from jax.experimental import pallas as pl
from jax.experimental.pallas import tpu as pltpu
from jax.sharding import PartitionSpec as P

MESH = pl.DeviceIdType.MESH
PANEL = 32
SUB = 16
CHUNK = 128


def split3(x):
    high = x.astype(jnp.bfloat16)
    rest = x - high.astype(jnp.float32)
    mid = rest.astype(jnp.bfloat16)
    low = (rest - mid.astype(jnp.float32)).astype(jnp.bfloat16)
    return high, mid, low


def small_inverse(cols):
    size = len(cols)
    row = lax.broadcasted_iota(jnp.int32, cols[0].shape, 0)
    cols = list(cols)
    for p in range(size):
        here = row == p
        inv = 1.0 / jnp.broadcast_to(cols[p][p : p + 1], cols[p].shape)
        factor = jnp.where(here, inv, -cols[p] * inv)
        for j in range(size):
            if j == p:
                cols[j] = factor
            else:
                pivot_row = jnp.broadcast_to(cols[j][p : p + 1], cols[j].shape)
                cols[j] = jnp.where(here, 0.0, cols[j]) + factor * pivot_row
    return cols


def combine(cols, rows):
    reps = rows.shape[1] // cols[0].shape[1]
    total = None
    for j, col in enumerate(cols):
        wide = jnp.concatenate([col] * reps, axis=1) if reps > 1 else col
        term = wide * jnp.broadcast_to(rows[j : j + 1], rows.shape)
        total = term if total is None else total + term
    return total


def eliminate(a_ref, k):
    n = a_ref.shape[0]
    base = pl.multiple_of(k * PANEL, PANEL)
    rows = a_ref[pl.ds(base, PANEL), :]
    lane = lax.broadcasted_iota(jnp.int32, (PANEL, n), 1)
    sub = lax.broadcasted_iota(jnp.int32, (PANEL, n), 0)
    inside = (lane >= base) & (lane < base + PANEL)
    eye = jnp.where(lane - base == sub, 1.0, 0.0)
    turned = jnp.where(inside, -eye, jnp.where(lane < base, -rows, rows))
    high, mid, low = split3(turned)
    left = jnp.concatenate([high, high, high, mid, mid, low], axis=0)
    rolled = pltpu.roll(rows, (n - base) % n, 1)
    count = PANEL // SUB
    panel = [rows[s * SUB : (s + 1) * SUB] for s in range(count)]
    diag = [rolled[s * SUB : (s + 1) * SUB, :128] for s in range(count)]
    lane_s, sub_s = lane[:SUB], sub[:SUB]
    lane_d = lax.broadcasted_iota(jnp.int32, (SUB, 128), 1)
    sub_d = lax.broadcasted_iota(jnp.int32, (SUB, 128), 0)
    for s in range(count):
        first = s * SUB
        cols = [
            [jnp.broadcast_to(diag[t][:, first + j : first + j + 1], (SUB, 128)) for j in range(SUB)]
            for t in range(count)
        ]
        inverse = small_inverse(cols[s])
        at = lane_s - base - first
        own = (at >= 0) & (at < SUB)
        at_d = lane_d - first
        own_d = (at_d >= 0) & (at_d < SUB)
        last = s + 1 == count
        fresh = combine(inverse, jnp.where(own, jnp.where(at == sub_s, 1.0, 0.0), panel[s]))
        fresh_d = None
        if not last:
            fresh_d = combine(inverse, jnp.where(own_d, jnp.where(at_d == sub_d, 1.0, 0.0), diag[s]))
        for t in range(count):
            if t != s:
                panel[t] = jnp.where(own, 0.0, panel[t]) - combine(cols[t], fresh)
                if not last:
                    diag[t] = jnp.where(own_d, 0.0, diag[t]) - combine(cols[t], fresh_d)
        panel[s] = fresh
        if not last:
            diag[s] = fresh_d
    solved = jnp.concatenate(panel, axis=0)
    high, mid, low = split3(solved)
    right = jnp.concatenate([high, mid, low, high, mid, high], axis=0)
    update = lax.dot_general(left, right, (((0,), (0,)), ((), ())), preferred_element_type=jnp.float32)
    lane_f = lax.broadcasted_iota(jnp.int32, (n, n), 1)
    a_ref[...] = jnp.where((lane_f >= base) & (lane_f < base + PANEL), 0.0, a_ref[...]) - update
    a_ref[pl.ds(base, PANEL), :] = solved


def block_product(block, item_id, word_id, items, words, item_rows):
    side = block.shape[0]
    rank = words.shape[1]
    item_rows[...] = items[pl.ds(item_id * side, side), :].astype(jnp.float32)
    word_rows = words[pl.ds(word_id * side, side), :]

    def step(c, total):
        terms = []
        for j in range(CHUNK):
            row = jnp.broadcast_to(item_rows[pl.ds(c * CHUNK + j, 1), :], (side, rank))
            terms.append(word_rows * row.astype(jnp.bfloat16))
        khatri = jnp.concatenate(terms, axis=0)
        values = block[:, pl.ds(pl.multiple_of(c * CHUNK * side, CHUNK * side), CHUNK * side)]
        return total + jnp.dot(values, khatri, preferred_element_type=jnp.float32)

    return lax.fori_loop(0, side // CHUNK, step, jnp.zeros((side, rank), jnp.float32))


def gram_of(rows):
    return lax.dot_general(rows, rows, (((0,), (0,)), ((), ())), preferred_element_type=jnp.float32)


def kernel(
    groups, owners, local_u,
    user_ids, item_ids, word_ids, blocks_hbm, item_hbm, word_hbm, out_ref,
    blocks, items, words, item_rows, part, gram, send, recv, mine, theirs, ids_send, ids_recv, select,
    block_sem, word_sem, item_sem, gather_send, gather_recv, pass_send, pass_recv,
    ids_ssem, ids_rsem, rows_ssem, rows_rsem, z_send, z_recv,
):
    nblocks, side = blocks.shape[0], blocks.shape[1]
    rank = words.shape[1]
    share = side // owners
    message = nblocks * share
    halves = rank // 128
    held = item_hbm.shape[0]
    half = held // 2
    group = lax.axis_index("blk")
    owner = lax.axis_index("own")
    core = owner % 2
    sibling = owner + 1 - 2 * core

    word_copy = pltpu.make_async_copy(word_hbm, words, word_sem)
    word_copy.start()
    mine_at = pl.multiple_of(group * held, held)
    item_copy = pltpu.make_async_copy(item_hbm, items.at[pl.ds(mine_at, held)], item_sem)
    item_copy.start()

    barrier = pltpu.get_barrier_semaphore()
    for d in range(1, groups):
        pl.semaphore_signal(barrier, inc=1, device_id=((group + d) % groups, owner), device_id_type=MESH)

    def greet(d, carry):
        pl.semaphore_signal(barrier, inc=1, device_id=(group, (owner + d) % owners), device_id_type=MESH)
        return carry

    lax.fori_loop(1, owners, greet, 0)
    for n in range(nblocks):
        pltpu.make_async_copy(blocks_hbm.at[n], blocks.at[n], block_sem.at[n]).start()
    pl.semaphore_wait(barrier, groups - 1 + owners - 1)

    quarter = half // 2
    pieces = ((1, 0, half), (3, 0, half), (2, 0, quarter), (2, quarter, quarter))

    def gather_copy(i):
        d, first, length = pieces[i]
        start = pl.multiple_of(group * held + core * half + first, quarter)
        return pltpu.make_async_remote_copy(
            src_ref=item_hbm.at[pl.ds(pl.multiple_of(core * half + first, quarter), length)],
            dst_ref=items.at[pl.ds(start, length)],
            send_sem=gather_send.at[i],
            recv_sem=gather_recv.at[i],
            device_id=((group + d) % groups, owner),
            device_id_type=MESH,
        )

    gathers = [gather_copy(i) for i in range(len(pieces))]
    for i in (2, 0, 1, 3):
        gathers[i].start()

    word_copy.wait()
    gram_words = gram_of(words[...])

    def pass_copy(i):
        d, first, length = pieces[i]
        start = pl.multiple_of((group + groups - d) % groups * held + core * half + first, quarter)
        return pltpu.make_async_remote_copy(
            src_ref=items.at[pl.ds(start, length)],
            dst_ref=items.at[pl.ds(start, length)],
            send_sem=pass_send.at[i],
            recv_sem=pass_recv.at[i],
            device_id=(group, sibling),
            device_id_type=MESH,
        )

    passes = [pass_copy(i) for i in range(len(pieces))]
    for gather, shared in zip(gathers, passes):
        gather.wait_recv()
        shared.start()

    for n in range(nblocks):
        ids_send[n * share : (n + 1) * share, :] = jnp.full((share, ids_send.shape[1]), user_ids[n], jnp.int32)
    own_ids = pltpu.make_async_copy(ids_send, ids_recv.at[owner], ids_rsem)
    own_ids.start()

    def send_ids(d, carry):
        pltpu.make_async_remote_copy(
            src_ref=ids_send, dst_ref=ids_recv.at[owner], send_sem=ids_ssem, recv_sem=ids_rsem,
            device_id=(group, (owner + d) % owners), device_id_type=MESH,
        ).start()
        return carry

    lax.fori_loop(1, owners, send_ids, 0)

    item_copy.wait()
    for shared in passes:
        shared.wait_recv()

    pair = 2 * share

    def row_copy(t, to):
        return pltpu.make_async_remote_copy(
            src_ref=send.at[:, pl.ds(pl.multiple_of(to * message + t * pair, pair), pair)],
            dst_ref=recv.at[:, pl.ds(pl.multiple_of(owner * message + t * pair, pair), pair)],
            send_sem=rows_ssem, recv_sem=rows_rsem,
            device_id=(group, to), device_id_type=MESH,
        )

    def product_step(n, carry):
        pltpu.make_async_copy(blocks_hbm.at[n], blocks.at[n], block_sem.at[n]).wait()
        product = block_product(blocks.at[n], item_ids[n], word_ids[n], items, words, item_rows)
        for h in range(halves):
            part[h] = product[:, h * 128 : (h + 1) * 128]
            for row in range(share):
                to_rows = pl.ds(n * share + row, owners, stride=message)
                send[h, to_rows, :] = part[h, pl.ds(row, owners, stride=share), :]

        @pl.when(n % 2 == 1)
        def _():
            def send_rows(d, inner):
                row_copy(n // 2, (owner + d) % owners).start()
                return inner

            lax.fori_loop(1, owners, send_rows, 0)

        return carry

    lax.fori_loop(0, nblocks, product_step, 0)
    mine_rows = pl.ds(pl.multiple_of(owner * message, message), message)
    pltpu.make_async_copy(send.at[:, mine_rows], recv.at[:, mine_rows], rows_rsem).start()

    pltpu.make_async_copy(ids_recv, ids_recv, ids_rsem).wait()
    rows_in = owners * message
    rows_out = groups * share * local_u
    ids = ids_recv[...].reshape(rows_in, ids_recv.shape[2])
    parts = []
    for h in range(rows_out // 128):
        to = lax.broadcasted_iota(jnp.int32, (rows_in, 128), 1) + h * 128
        source = lax.broadcasted_iota(jnp.int32, (rows_in, 128), 0)
        to_user = to // (share * local_u) * local_u + to % local_u
        hit = (ids == to_user) & (source % share == to // local_u % share)
        parts.append(jnp.where(hit, 1.0, 0.0).astype(jnp.bfloat16))
    select[...] = jnp.concatenate(parts, axis=1).T

    gram[...] = gram_of(items[...]) * gram_words
    steps = rank // PANEL

    def eliminate_step(k, carry):
        eliminate(gram, k)
        return carry

    lax.fori_loop(0, steps // 2, eliminate_step, 0)

    pltpu.make_async_copy(recv, recv, rows_rsem).wait()
    high, mid, low = split3(jnp.concatenate([recv[h] for h in range(halves)], axis=1))
    chosen = select[...]
    total = jnp.dot(chosen, high, preferred_element_type=jnp.float32)
    total += jnp.dot(chosen, mid, preferred_element_type=jnp.float32)
    total += jnp.dot(chosen, low, preferred_element_type=jnp.float32)
    mine[...] = total
    count = share * local_u

    def z_copy(d):
        to = (group + d) % groups
        return pltpu.make_async_remote_copy(
            src_ref=mine.at[pl.ds(pl.multiple_of(to * count, count), count)],
            dst_ref=theirs.at[d - 1],
            send_sem=z_send.at[d - 1], recv_sem=z_recv.at[d - 1],
            device_id=(to, owner), device_id_type=MESH,
        )

    zs = [z_copy(d) for d in range(1, groups)]
    for z in zs:
        z.start()

    lax.fori_loop(steps // 2, steps, eliminate_step, 0)

    rows = mine[pl.ds(pl.multiple_of(group * count, count), count), :]
    for d in range(1, groups):
        zs[d - 1].wait_recv()
        rows = rows + theirs[d - 1]
    solved = jnp.dot(rows, gram[...], preferred_element_type=jnp.float32, precision=lax.Precision.HIGHEST)
    out_ref[...] = solved.reshape(out_ref.shape)

    for sent in gathers + passes + zs:
        sent.wait_send()
    other_ids = ids_recv.at[pl.ds(0, owners - 1)]
    pltpu.make_async_copy(other_ids, other_ids, ids_ssem).wait()
    other_rows = send.at[:, pl.ds(0, (owners - 1) * message)]
    pltpu.make_async_copy(other_rows, other_rows, rows_ssem).wait()


def solution(mesh):
    groups, owners = mesh.shape["blk"], mesh.shape["own"]

    def on_device(blocks, user_block, item_block, word_block, item_factor, word_factor):
        nblocks, side, _ = blocks.shape
        rank = item_factor.shape[1]
        share = side // owners
        message = nblocks * share
        local_u = nblocks * owners // 8
        count = share * local_u
        dma = pltpu.SemaphoreType.DMA
        smem = pl.BlockSpec(memory_space=pltpu.SMEM)
        hbm = pl.BlockSpec(memory_space=pl.ANY)
        return pl.pallas_call(
            functools.partial(kernel, groups, owners, local_u),
            out_shape=jax.ShapeDtypeStruct((share, local_u, rank), jnp.float32),
            in_specs=[smem, smem, smem, hbm, hbm, hbm],
            out_specs=pl.BlockSpec(memory_space=pltpu.VMEM),
            scratch_shapes=[
                pltpu.VMEM(blocks.shape, jnp.bfloat16),
                pltpu.VMEM((groups * item_factor.shape[0], rank), jnp.bfloat16),
                pltpu.VMEM(word_factor.shape, jnp.bfloat16),
                pltpu.VMEM((side, rank), jnp.float32),
                pltpu.VMEM((rank // 128, side, 128), jnp.float32),
                pltpu.VMEM((rank, rank), jnp.float32),
                pltpu.VMEM((rank // 128, owners * message, 128), jnp.float32),
                pltpu.VMEM((rank // 128, owners * message, 128), jnp.float32),
                pltpu.VMEM((groups * count, rank), jnp.float32),
                pltpu.VMEM((groups - 1, count, rank), jnp.float32),
                pltpu.VMEM((message, 128), jnp.int32),
                pltpu.VMEM((owners, message, 128), jnp.int32),
                pltpu.VMEM((groups * count, owners * message), jnp.bfloat16),
                dma((nblocks,)), dma, dma,
                dma((4,)), dma((4,)), dma((4,)), dma((4,)),
                dma, dma, dma, dma,
                dma((groups - 1,)), dma((groups - 1,)),
            ],
            compiler_params=pltpu.CompilerParams(
                collective_id=0, has_side_effects=True, vmem_limit_bytes=56 * 2**20
            ),
            name="als_user_update",
        )(user_block, item_block, word_block, blocks, item_factor, word_factor)

    return jax.shard_map(
        on_device,
        mesh=mesh,
        in_specs=(
            P(("blk", "own"), None, None),
            P(("blk", "own")),
            P(("blk", "own")),
            P(("blk", "own")),
            P("blk", None),
            P(),
        ),
        out_specs=P("own", "blk", None),
        check_vma=False,
    )
```
